32 devices in a mesh: gx: 2 (over y), gy: 4 (over z), gz: 4 (over x, core).
Axes of the slice: x: 2, y: 2, z: 4, core: 2. Of those that a mesh axis runs over, the one named last changes fastest.
Arguments:
- field: float32 [4, 512, 16, 512], P('gx', 'gy', None, 'gz'), may hold values from -45 to 45
- start_basis: float32 [512, 128], replicated, may hold values from -6 to 6
Outputs:
- factor_out: float32 [512, 512], P('gy', 'gz')
- core: float32 [4, 128, 16, 512], P('gx', 'gy', None, 'gz')
The draws below stay inside these ranges and needn't reach their ends.
All inputs are finite; a program needn't handle non-finite values.
Results may differ from the reference program's by a relative error of at most 0.0003.
Values sent between devices are 32-bit elements; how exact they have to be, the bound alone decides.
A program may use at most 64 MiB of HBM per device.

```python
import jax
import jax.numpy as jnp
from jax import lax

NY = 512
RANK = 128
NS = 16
ITERS = 2
NX = 4
NZ = 512


def draw_field(key, part):
    keys = jax.random.split(key, 2)
    planes = jnp.arange(NX, dtype=jnp.float32)
    rising = 3.0 ** (planes / max(NX - 1, 1))
    plane_scale = jnp.exp(jax.random.uniform(keys[0], (NX, NY, NS, 1), jnp.float32) * jnp.log(10.0))
    plane_scale = plane_scale * rising[:, None, None, None] * 0.25
    shape = (NX, NY, NS, NZ)
    values = plane_scale * jnp.clip(jax.random.normal(keys[1], shape, jnp.float32), -6.0, 6.0)
    return values


def scatter_about(key, dims, scale, most, kind=jnp.bfloat16):
    return jnp.clip(scale * jax.random.normal(key, dims, jnp.float32), -most, most).astype(kind)


def setup_inputs(seed: int = 0) -> dict:
    streams_of = jax.random.split(jax.random.key(seed), 3)
    field = draw_field(jax.random.fold_in(streams_of[2], 71), 0)
    start_basis = scatter_about(streams_of[1], (NY, RANK), 1.0, 6.0, jnp.float32)
    return {"field": field, "start_basis": start_basis}


def add_plane(total, plane):
    return (total + jnp.einsum('ysz,wsz->yw', plane, plane, precision=lax.Precision.HIGHEST), None)

def reference(field, start_basis):
    gram, unused = lax.scan(add_plane, jnp.zeros((NY, NY), jnp.float32), field)
    lower = jnp.linalg.cholesky(gram)
    factor_out = lower / jnp.sqrt(jnp.float32(NX * NS * NZ))
    basis = start_basis
    for step in range(ITERS):
        inner = jnp.dot(lower.T, basis, precision=lax.Precision.HIGHEST)
        wide = jnp.dot(lower, inner, precision=lax.Precision.HIGHEST)
        chol = jnp.linalg.cholesky(jnp.dot(wide.T, wide, precision=lax.Precision.HIGHEST))
        basis = jax.scipy.linalg.solve_triangular(chol, wide.T, lower=True).T
    core = jnp.einsum('yr,xysz->xrsz', basis, field, precision=lax.Precision.HIGHEST)
    return (factor_out, core)
```

```python
import functools

import jax
import jax.numpy as jnp
from jax import lax
from jax.experimental import pallas as pl
from jax.experimental.pallas import tpu as pltpu
from jax.sharding import PartitionSpec as P

ITERS = 2
B = 128
MESH = pl.DeviceIdType.MESH
VMEM = pl.BlockSpec(memory_space=pltpu.VMEM)
ANY = pl.BlockSpec(memory_space=pl.ANY)
F32 = jnp.float32
BF16 = jnp.bfloat16


def pieces(a):
    hi = a.astype(BF16)
    return hi, (a - hi.astype(F32)).astype(BF16)


def dot3(a, b, ca, cb):
    ah, al = pieces(a)
    bh, bl = pieces(b)
    return lax.dot_general(
        jnp.concatenate([ah, ah, al], axis=ca),
        jnp.concatenate([bh, bl, bh], axis=cb),
        (((ca,), (cb,)), ((), ())),
        preferred_element_type=F32,
    )


def upper(nb):
    return [(i, j) for i in range(nb) for j in range(i, nb)]


def gram_kernel(sizes, field, full, reg, part, gram, tmp_c, tmp_x, tmp_g, tmp_y, sems, ssem, rsem, lsem):
    n_gx, n_gy, n_gz = sizes
    gx, gy, gz = (lax.axis_index(a) for a in ("gx", "gy", "gz"))
    planes, rows = field.shape[0], field.shape[1]
    quarter = field.shape[2] // n_gy
    chunks = planes * quarter
    nb = gram.shape[0] // B

    def peer(axis, index):
        where = {"gx": gx, "gy": gy, "gz": gz}
        where[axis] = index
        return (where["gx"], where["gy"], where["gz"])

    core = lax.rem(gz, 2)
    other_core = gz + 1 - 2 * core
    half = lax.div(gz, 2)
    other_half = gz + 2 - 4 * half
    y_peers = [lax.rem(gy + k, n_gy) for k in range(1, n_gy)]
    x_peers = [lax.rem(gx + k, n_gx) for k in range(1, n_gx)]
    greet = [peer("gy", d) for d in y_peers] + [peer("gx", d) for d in x_peers]
    greet += [peer("gz", other_core), peer("gz", other_half)]
    barrier = pltpu.get_barrier_semaphore()
    for who in greet:
        pl.semaphore_signal(barrier, inc=1, device_id=who, device_id_type=MESH)
    pl.semaphore_wait(barrier, len(greet))

    mine = pl.ds(pl.multiple_of(gy * rows, rows), rows)

    def send(c, k):
        x, s = c // quarter, c % quarter
        d = y_peers[k]
        return pltpu.make_async_remote_copy(
            src_ref=field.at[x, :, d * quarter + s, :],
            dst_ref=reg.at[c, mine, :],
            send_sem=ssem.at[c, k],
            recv_sem=rsem.at[c, k],
            device_id=peer("gy", d),
            device_id_type=MESH,
        )

    def keep(c):
        x, s = c // quarter, c % quarter
        return pltpu.make_async_copy(
            field.at[x, :, gy * quarter + s, :], reg.at[c, mine, :], lsem.at[c]
        )

    @pl.loop(0, chunks)
    def _(c):
        for k in range(n_gy - 1):
            send(c, k).start()
        keep(c).start()

    gram[...] = jnp.zeros_like(gram)

    @pl.loop(0, chunks)
    def _(c):
        for k in range(n_gy - 1):
            send(c, k).wait()
        keep(c).wait()
        f = reg[c]
        gram[...] += dot3(f, f, 1, 1)

    for b, (i, j) in enumerate(upper(nb)):
        part[b * B:(b + 1) * B, :] = gram[i * B:(i + 1) * B, j * B:(j + 1) * B]

    def swap(src, dst, s, who):
        return pltpu.make_async_remote_copy(
            src_ref=src, dst_ref=dst, send_sem=sems.at[0, s], recv_sem=sems.at[1, s],
            device_id=who, device_id_type=MESH,
        )

    def span(start, size):
        return pl.ds(pl.multiple_of(start, 8), size)

    total = part.shape[0]
    s = 0
    n_c = total // 2
    keep_c = core * n_c
    cp = swap(part.at[span(n_c - keep_c, n_c), :], tmp_c, s, peer("gz", other_core))
    cp.start()
    cp.wait()
    s += 1
    part[span(keep_c, n_c), :] += tmp_c[...]
    n_x = n_c // 2
    keep_x = keep_c + half * n_x
    cp = swap(part.at[span(keep_c + n_x - half * n_x, n_x), :], tmp_x, s, peer("gz", other_half))
    cp.start()
    cp.wait()
    s += 1
    part[span(keep_x, n_x), :] += tmp_x[...]
    n_g = n_x // n_gx
    keep_g = keep_x + gx * n_g
    cps = []
    for k, d in enumerate(x_peers):
        cp = swap(part.at[span(keep_x + d * n_g, n_g), :], tmp_g.at[k], s, peer("gx", d))
        cp.start()
        cps.append(cp)
        s += 1
    for cp in cps:
        cp.wait()
    acc = part[span(keep_g, n_g), :]
    for k in range(n_gx - 1):
        acc += tmp_g[k]
    part[span(keep_g, n_g), :] = acc
    cps = []
    for k, d in enumerate(y_peers):
        cp = swap(part.at[span(keep_g, n_g), :], tmp_y.at[k], s, peer("gy", d))
        cp.start()
        cps.append(cp)
        s += 1
    for cp in cps:
        cp.wait()
    acc = part[span(keep_g, n_g), :]
    for k in range(n_gy - 1):
        acc += tmp_y[k]
    full[span(keep_g, n_g), :] = acc
    cps = []
    for k, d in enumerate(x_peers):
        here = full.at[span(keep_g, n_g), :]
        cp = swap(here, here, s, peer("gx", d))
        cp.start()
        cps.append(cp)
        s += 1
    for cp in cps:
        cp.wait()
    here = full.at[span(keep_x, n_x), :]
    cp = swap(here, here, s, peer("gz", other_half))
    cp.start()
    cp.wait()
    s += 1
    here = full.at[span(keep_c, n_c), :]
    cp = swap(here, here, s, peer("gz", other_core))
    cp.start()
    cp.wait()


def factor_blocks(refs):
    sub = lax.broadcasted_iota(jnp.int32, (8, B), 0)
    for p in range(B // 8):
        lo = 8 * p
        for ref in refs:
            a = ref[lo:lo + 8, :B]
            e = ref[lo:lo + 8, B:]
            cols = [jnp.broadcast_to(a[:, lo + k:lo + k + 1], (8, B)) for k in range(8)]
            for j in range(8):
                r = lax.rsqrt(cols[j][j:j + 1])
                coef = jnp.where(sub > j, cols[j] * r, 0.0)
                ua, ue = a[j:j + 1] * r, e[j:j + 1] * r
                a = jnp.where(sub == j, ua, a - coef * ua)
                e = jnp.where(sub == j, ue, e - coef * ue)
                for k in range(j + 1, 8):
                    cols[k] = cols[k] - coef * (cols[k][j:j + 1] * r)
            ref[lo:lo + 8, :B] = a
            ref[lo:lo + 8, B:] = e
            if lo + 8 < B:
                u = jnp.concatenate([a, e], axis=1)
                ah = a.astype(BF16).astype(F32)
                al = a - ah
                uh = u.astype(BF16).astype(F32)
                ul = u - uh
                lhs = jnp.concatenate([ah, ah, al, al], axis=0).astype(BF16)
                rhs = jnp.concatenate([uh, ul, uh, ul], axis=0).astype(BF16)
                down = lax.dot_general(
                    lhs, rhs, (((0,), (0,)), ((), ())), preferred_element_type=F32
                )
                ref[lo + 8:, :] -= down[lo + 8:]


def solve_kernel(columns, packed, start, factor, basis_t, g, r, m_g, m_s):
    n = g.shape[0]
    nb = n // B
    row = lax.broadcasted_iota(jnp.int32, (B, B), 0)
    col = lax.broadcasted_iota(jnp.int32, (B, B), 1)
    eye = jnp.where(row == col, 1.0, 0.0).astype(F32)
    for b, (i, j) in enumerate(upper(nb)):
        block = packed[b * B:(b + 1) * B, :]
        g[i * B:(i + 1) * B, j * B:(j + 1) * B] = block
        if i != j:
            g[j * B:(j + 1) * B, i * B:(i + 1) * B] = block.T
        r[i * B:(i + 1) * B, j * B:(j + 1) * B] = block
    basis_t[...] = start[...].T
    for step in range(max(nb, ITERS)):
        refs = []
        if step < nb:
            lo, hi = step * B, (step + 1) * B
            m_g[:, :B] = r[lo:hi, lo:hi]
            m_g[:, B:] = eye
            refs.append(m_g)
        if step < ITERS:
            wide_t = dot3(basis_t[...], g[...], 1, 0)
            m_s[:, :B] = dot3(wide_t, wide_t, 1, 1)
            m_s[:, B:] = eye
            refs.append(m_s)
        factor_blocks(refs)
        if step < ITERS:
            basis_t[...] = dot3(jnp.where(row >= col, m_s[:, B:], 0.0), wide_t, 1, 0)
        if step < nb:
            r[lo:hi, lo:hi] = jnp.where(row <= col, m_g[:, :B], 0.0)
            if step + 1 < nb:
                u = dot3(jnp.where(row >= col, m_g[:, B:], 0.0), r[lo:hi, hi:], 1, 0)
                r[lo:hi, hi:] = u
                r[hi:, hi:] -= dot3(u, u, 0, 0)
    gy, gz = lax.axis_index("gy"), lax.axis_index("gz")
    scale = 1.0 / jnp.sqrt(F32(columns))
    factor[...] = jnp.zeros_like(factor)
    for i, j in upper(nb):
        @pl.when((gy == j) & (gz == i))
        def _():
            factor[...] = r[i * B:(i + 1) * B, j * B:(j + 1) * B].T * scale


def core_kernel(n_gy, basis_t, reg, core, proj, ssem, rsem, lsem):
    gx, gy, gz = (lax.axis_index(a) for a in ("gx", "gy", "gz"))
    peers = [lax.rem(gy + k, n_gy) for k in range(1, n_gy)]
    barrier = pltpu.get_barrier_semaphore()
    for d in peers:
        pl.semaphore_signal(barrier, inc=1, device_id=(gx, d, gz), device_id_type=MESH)
    planes, kept = core.shape[0], core.shape[2]
    quarter = core.shape[1] // n_gy
    mine = pl.ds(gy * quarter, quarter)
    bh, bl = pieces(basis_t[...])
    left = jnp.concatenate([bh, bh, bl], axis=1)
    cps = []
    for x in range(planes):
        for s in range(quarter):
            fh, fl = pieces(reg[x * quarter + s])
            res = jnp.dot(left, jnp.concatenate([fh, fl, fh], axis=0), preferred_element_type=F32)
            for d in range(n_gy):
                proj[d, x, s] = res[d * kept:(d + 1) * kept]
        if x == 0:
            pl.semaphore_wait(barrier, n_gy - 1)
        for k, d in enumerate(peers):
            cp = pltpu.make_async_remote_copy(
                src_ref=proj.at[d, x], dst_ref=core.at[x, mine], send_sem=ssem.at[x, k],
                recv_sem=rsem.at[x, k], device_id=(gx, d, gz), device_id_type=MESH,
            )
            cp.start()
            cps.append(cp)
        cp = pltpu.make_async_copy(proj.at[gy, x], core.at[x, mine], lsem.at[x])
        cp.start()
        cps.append(cp)
    for cp in cps:
        cp.wait()


def per_device(sizes, field, start_basis):
    n_gx, n_gy, n_gz = sizes
    planes, rows, species, width = field.shape
    n, rank = start_basis.shape
    quarter = species // n_gy
    chunks = planes * quarter
    nb = n // B
    total = len(upper(nb)) * B
    columns = planes * n_gx * species * width * n_gz
    n_g = total // 4 // n_gx
    n_sems = 2 + 2 * (n_gx - 1) + (n_gy - 1) + 2
    packed, reg = pl.pallas_call(
        functools.partial(gram_kernel, sizes),
        out_shape=(
            jax.ShapeDtypeStruct((total, B), F32),
            jax.ShapeDtypeStruct((chunks, n, width), F32),
        ),
        in_specs=[ANY],
        out_specs=(VMEM, VMEM),
        scratch_shapes=[
            pltpu.VMEM((total, B), F32),
            pltpu.VMEM((n, n), F32),
            pltpu.VMEM((total // 2, B), F32),
            pltpu.VMEM((total // 4, B), F32),
            pltpu.VMEM((max(n_gx - 1, 1), n_g, B), F32),
            pltpu.VMEM((n_gy - 1, n_g, B), F32),
            pltpu.SemaphoreType.DMA((2, n_sems)),
            pltpu.SemaphoreType.DMA((chunks, n_gy - 1)),
            pltpu.SemaphoreType.DMA((chunks, n_gy - 1)),
            pltpu.SemaphoreType.DMA((chunks,)),
        ],
        compiler_params=pltpu.CompilerParams(
            collective_id=0, has_side_effects=True, vmem_limit_bytes=32 << 20
        ),
        name="gram",
    )(field)
    factor, basis_t = pl.pallas_call(
        functools.partial(solve_kernel, columns),
        out_shape=(
            jax.ShapeDtypeStruct((n // n_gy, n // n_gz), F32),
            jax.ShapeDtypeStruct((rank, n), F32),
        ),
        in_specs=[VMEM, VMEM],
        out_specs=(VMEM, VMEM),
        scratch_shapes=[
            pltpu.VMEM((n, n), F32),
            pltpu.VMEM((n, n), F32),
            pltpu.VMEM((B, 2 * B), F32),
            pltpu.VMEM((B, 2 * B), F32),
        ],
        compiler_params=pltpu.CompilerParams(vmem_limit_bytes=32 << 20),
        name="solve",
    )(packed, start_basis)
    core = pl.pallas_call(
        functools.partial(core_kernel, n_gy),
        out_shape=jax.ShapeDtypeStruct((planes, species, rank // n_gy, width), F32),
        in_specs=[VMEM, VMEM],
        out_specs=VMEM,
        scratch_shapes=[
            pltpu.VMEM((n_gy, planes, quarter, rank // n_gy, width), F32),
            pltpu.SemaphoreType.DMA((planes, n_gy - 1)),
            pltpu.SemaphoreType.DMA((planes, n_gy - 1)),
            pltpu.SemaphoreType.DMA((planes,)),
        ],
        compiler_params=pltpu.CompilerParams(
            collective_id=1, has_side_effects=True, vmem_limit_bytes=32 << 20
        ),
        name="core",
    )(basis_t, reg)
    return factor, jnp.transpose(core, (0, 2, 1, 3))


def solution(mesh):
    sizes = tuple(mesh.shape[a] for a in ("gx", "gy", "gz"))
    return jax.shard_map(
        functools.partial(per_device, sizes),
        mesh=mesh,
        in_specs=(P("gx", "gy", None, "gz"), P()),
        out_specs=(P("gy", "gz"), P("gx", "gy", None, "gz")),
        check_vma=False,
    )
```

```python
import functools

import jax
import jax.numpy as jnp
from jax import lax
from jax.experimental import pallas as pl
from jax.experimental.pallas import tpu as pltpu
from jax.sharding import PartitionSpec as P

ITERS = 2
B = 128
MESH = pl.DeviceIdType.MESH
VMEM = pl.BlockSpec(memory_space=pltpu.VMEM)
HBM = pl.BlockSpec(memory_space=pltpu.HBM)
F32 = jnp.float32
BF16 = jnp.bfloat16


def pieces(a):
    hi = a.astype(BF16)
    return hi, (a - hi.astype(F32)).astype(BF16)


def dot3(a, b, ca, cb):
    ah, al = pieces(a)
    bh, bl = pieces(b)
    return lax.dot_general(
        jnp.concatenate([ah, ah, al], axis=ca),
        jnp.concatenate([bh, bl, bh], axis=cb),
        (((ca,), (cb,)), ((), ())),
        preferred_element_type=F32,
    )


def above(nb):
    return [(i, j) for i in range(nb) for j in range(i + 1, nb)]


def upper(nb):
    return [(i, j) for i in range(nb) for j in range(i, nb)]


def gram_kernel(
    sizes, field, full, full_d, reg, part, gram, tmp_c, tmp_g, tmp_y,
    own, diag, part_d, tmp_dc, tmp_dg, sems, ssem, rsem, lsem, osem,
):
    n_gx, n_gy, n_gz = sizes
    gx, gy, gz = (lax.axis_index(a) for a in ("gx", "gy", "gz"))
    planes, rows = field.shape[0], field.shape[1]
    quarter = field.shape[2] // n_gy
    chunks = planes * quarter
    nb = gram.shape[0] // B

    def peer(axis, index):
        where = {"gx": gx, "gy": gy, "gz": gz}
        where[axis] = index
        return (where["gx"], where["gy"], where["gz"])

    core = lax.rem(gz, 2)
    other_core = gz + 1 - 2 * core
    half = lax.div(gz, 2)
    y_peers = [lax.rem(gy + k, n_gy) for k in range(1, n_gy)]
    offsets = [(dx, dg) for dx in range(2) for dg in range(n_gx) if dx or dg]
    plane = []
    for dx, dg in offsets:
        h, g = lax.rem(half + dx, 2), lax.rem(gx + dg, n_gx)
        plane.append((h, g, (g, gy, 2 * h + core)))
    greet = [peer("gy", d) for d in y_peers] + [who for _, _, who in plane]
    greet.append(peer("gz", other_core))
    barrier = pltpu.get_barrier_semaphore()
    for who in greet:
        pl.semaphore_signal(barrier, inc=1, device_id=who, device_id_type=MESH)
    pl.semaphore_wait(barrier, len(greet))

    mine = pl.ds(pl.multiple_of(gy * rows, rows), rows)

    def send(c, k):
        x, s = c // quarter, c % quarter
        d = y_peers[k]
        return pltpu.make_async_remote_copy(
            src_ref=field.at[x, :, d * quarter + s, :],
            dst_ref=reg.at[c, mine, :],
            send_sem=ssem.at[c, k],
            recv_sem=rsem.at[c, k],
            device_id=peer("gy", d),
            device_id_type=MESH,
        )

    def keep(c):
        x, s = c // quarter, c % quarter
        return pltpu.make_async_copy(
            field.at[x, :, gy * quarter + s, :], reg.at[c, mine, :], lsem.at[c]
        )

    @pl.loop(0, chunks)
    def _(c):
        for k in range(n_gy - 1):
            send(c, k).start()
        keep(c).start()

    def keep_own(q):
        species = field.shape[2]
        return pltpu.make_async_copy(
            field.at[q // species, :, q % species, :], own.at[q], osem.at[q]
        )

    @pl.loop(0, own.shape[0])
    def _(q):
        keep_own(q).start()

    used = [0]

    def swap(src, dst, who):
        s = used[0]
        used[0] += 1
        cp = pltpu.make_async_remote_copy(
            src_ref=src, dst_ref=dst, send_sem=sems.at[0, s], recv_sem=sems.at[1, s],
            device_id=who, device_id_type=MESH,
        )
        cp.start()
        return cp

    def span(start, size):
        return pl.ds(pl.multiple_of(start, 8), size)

    partner = peer("gz", other_core)

    diag[...] = jnp.zeros_like(diag)

    @pl.loop(0, own.shape[0])
    def _(q):
        keep_own(q).wait()
        f = own[q]
        diag[...] += dot3(f, f, 1, 1)

    n_p = 2 * n_gx
    rows_d = part_d.shape[1]
    for p in range(2 * n_p):
        part_d[p] = diag[p * rows_d:(p + 1) * rows_d]
    cp = swap(part_d.at[pl.ds((1 - core) * n_p, n_p)], tmp_dc, partner)
    cp.wait()
    for p in range(n_p):
        part_d[core * n_p + p] += tmp_dc[p]
    cps = []
    for k, (h, g, who) in enumerate(plane):
        cps.append(swap(part_d.at[core * n_p + h * n_gx + g], tmp_dg.at[k], who))
    for cp in cps:
        cp.wait()
    mine_d = core * n_p + half * n_gx + gx
    acc = part_d[mine_d]
    for k in range(len(plane)):
        acc += tmp_dg[k]
    full_d[gy, mine_d] = acc
    diag_cps = []
    for d in y_peers:
        here = full_d.at[gy, mine_d]
        diag_cps.append(swap(here, here, peer("gy", d)))

    gram[...] = jnp.zeros_like(gram)

    @pl.loop(0, chunks)
    def _(c):
        for k in range(n_gy - 1):
            send(c, k).wait()
        keep(c).wait()
        f = reg[c]
        gram[...] += dot3(f, f, 1, 1)

    for b, (i, j) in enumerate(above(nb)):
        part[b * B:(b + 1) * B, :] = gram[i * B:(i + 1) * B, j * B:(j + 1) * B]

    total = part.shape[0]
    n_c = total // 2
    keep_c = core * n_c
    cp = swap(part.at[span(n_c - keep_c, n_c), :], tmp_c, partner)
    cp.wait()
    part[span(keep_c, n_c), :] += tmp_c[...]
    n_g = n_c // n_p

    def piece(h, g):
        return span(keep_c + (h * n_gx + g) * n_g, n_g)

    mine_g = piece(half, gx)
    cps = []
    for k, (h, g, who) in enumerate(plane):
        cps.append(swap(part.at[piece(h, g), :], tmp_g.at[k], who))
    for cp in diag_cps:
        cp.wait()
    for cp in cps:
        cp.wait()
    acc = part[mine_g, :]
    for k in range(len(plane)):
        acc += tmp_g[k]
    part[mine_g, :] = acc
    cps = []
    for k, d in enumerate(y_peers):
        cps.append(swap(part.at[mine_g, :], tmp_y.at[k], peer("gy", d)))
    here = full_d.at[:, mine_d]
    plane_d = [swap(here, here, who) for _, _, who in plane]
    onward = [swap(here, here, partner)]
    came_from = []
    for dx, dg in offsets:
        h = lax.rem(half + 2 - dx, 2)
        g = lax.rem(gx + n_gx - dg, n_gx)
        came_from.append((h, g))
    for cp, (h, g) in zip(plane_d, came_from):
        cp.wait_recv()
        here = full_d.at[:, core * n_p + h * n_gx + g]
        onward.append(swap(here, here, partner))
    for cp in cps:
        cp.wait()
    acc = part[mine_g, :]
    for k in range(n_gy - 1):
        acc += tmp_y[k]
    full[mine_g, :] = acc
    here = full.at[mine_g, :]
    cps = [swap(here, here, who) for _, _, who in plane]
    onward.append(swap(here, here, partner))
    for cp, (h, g) in zip(cps, came_from):
        cp.wait_recv()
        here = full.at[piece(h, g), :]
        onward.append(swap(here, here, partner))
    for cp in plane_d + cps:
        cp.wait_send()
    for cp in onward:
        cp.wait()


PANEL = 16


def factor_blocks(refs):
    sub = lax.broadcasted_iota(jnp.int32, (PANEL, B), 0)
    for lo in range(0, B, PANEL):
        for ref in refs:
            a = ref[lo:lo + PANEL, :B]
            e = ref[lo:lo + PANEL, B:]
            cols = [jnp.broadcast_to(a[:, lo + k:lo + k + 1], (PANEL, B)) for k in range(PANEL)]
            for j in range(PANEL):
                r = lax.rsqrt(cols[j][j:j + 1])
                coef = jnp.where(sub > j, cols[j] * r, 0.0)
                ua, ue = a[j:j + 1] * r, e[j:j + 1] * r
                a = jnp.where(sub == j, ua, a - coef * ua)
                e = jnp.where(sub == j, ue, e - coef * ue)
                for k in range(j + 1, PANEL):
                    cols[k] = cols[k] - coef * (cols[k][j:j + 1] * r)
            ref[lo:lo + PANEL, :B] = a
            ref[lo:lo + PANEL, B:] = e
            if lo + PANEL < B:
                u = jnp.concatenate([a, e], axis=1)
                ah = a.astype(BF16).astype(F32)
                al = a - ah
                uh = u.astype(BF16).astype(F32)
                ul = u - uh
                lhs = jnp.concatenate([ah, ah, al, al], axis=0).astype(BF16)
                rhs = jnp.concatenate([uh, ul, uh, ul], axis=0).astype(BF16)
                down = lax.dot_general(
                    lhs, rhs, (((0,), (0,)), ((), ())), preferred_element_type=F32
                )
                ref[lo + PANEL:, :] -= down[lo + PANEL:]


def triangles():
    row = lax.broadcasted_iota(jnp.int32, (B, B), 0)
    col = lax.broadcasted_iota(jnp.int32, (B, B), 1)
    return row, col, jnp.where(row == col, 1.0, 0.0).astype(F32)


def load_block(step, r, m_g, eye):
    lo, hi = step * B, (step + 1) * B
    m_g[:, :B] = r[lo:hi, lo:hi]
    m_g[:, B:] = eye


def finish_block(step, r, m_g, row, col):
    lo, hi = step * B, (step + 1) * B
    r[lo:hi, lo:hi] = jnp.where(row <= col, m_g[:, :B], 0.0)
    if hi < r.shape[0]:
        u = dot3(jnp.where(row >= col, m_g[:, B:], 0.0), r[lo:hi, hi:], 1, 0)
        r[lo:hi, hi:] = u
        r[hi:, hi:] -= dot3(u, u, 0, 0)


def basis_kernel(packed, diagonal, start, basis_t, r, g, m_g, m_s):
    nb = r.shape[0] // B
    row, col, eye = triangles()
    for b, (i, j) in enumerate(above(nb)):
        block = packed[b * B:(b + 1) * B, :]
        g[i * B:(i + 1) * B, j * B:(j + 1) * B] = block
        g[j * B:(j + 1) * B, i * B:(i + 1) * B] = block.T
        r[i * B:(i + 1) * B, j * B:(j + 1) * B] = block
        r[j * B:(j + 1) * B, i * B:(i + 1) * B] = jnp.zeros_like(block)
    rows = diagonal.shape[2]
    for i in range(nb):
        for p in range(B // rows):
            there = slice(i * B + p * rows, i * B + (p + 1) * rows)
            g[there, i * B:(i + 1) * B] = diagonal[i, p]
            r[there, i * B:(i + 1) * B] = diagonal[i, p]
    basis_t[...] = start[...].T
    for step in range(ITERS):
        load_block(step, r, m_g, eye)
        wide_t = dot3(basis_t[...], g[...], 1, 0)
        m_s[:, :B] = dot3(wide_t, wide_t, 1, 1)
        m_s[:, B:] = eye
        factor_blocks([m_s, m_g])
        basis_t[...] = dot3(jnp.where(row >= col, m_s[:, B:], 0.0), wide_t, 1, 0)
        finish_block(step, r, m_g, row, col)


def core_kernel(n_gy, columns, basis_t, reg, started, core, factor, r, m_g, proj, ssem, rsem, lsem):
    gx, gy, gz = (lax.axis_index(a) for a in ("gx", "gy", "gz"))
    peers = [lax.rem(gy + k, n_gy) for k in range(1, n_gy)]
    barrier = pltpu.get_barrier_semaphore()
    for d in peers:
        pl.semaphore_signal(barrier, inc=1, device_id=(gx, d, gz), device_id_type=MESH)
    planes, kept = core.shape[0], core.shape[2]
    quarter = core.shape[1] // n_gy
    mine = pl.ds(gy * quarter, quarter)
    bh, bl = pieces(basis_t[...])
    left = jnp.concatenate([bh, bh, bl], axis=1)
    cps = []
    for x in range(planes):
        for s in range(quarter):
            fh, fl = pieces(reg[x * quarter + s])
            res = jnp.dot(left, jnp.concatenate([fh, fl, fh], axis=0), preferred_element_type=F32)
            for d in range(n_gy):
                proj[d, x, s] = res[d * kept:(d + 1) * kept]
        if x == 0:
            pl.semaphore_wait(barrier, n_gy - 1)
        for k, d in enumerate(peers):
            cp = pltpu.make_async_remote_copy(
                src_ref=proj.at[d, x], dst_ref=core.at[x, mine], send_sem=ssem.at[x, k],
                recv_sem=rsem.at[x, k], device_id=(gx, d, gz), device_id_type=MESH,
            )
            cp.start()
            cps.append(cp)
        cp = pltpu.make_async_copy(proj.at[gy, x], core.at[x, mine], lsem.at[x])
        cp.start()
        cps.append(cp)
    row, col, eye = triangles()
    r[...] = started[...]
    nb = r.shape[0] // B
    for step in range(ITERS, nb):
        load_block(step, r, m_g, eye)
        factor_blocks([m_g])
        finish_block(step, r, m_g, row, col)
    scale = 1.0 / jnp.sqrt(F32(columns))
    factor[...] = jnp.zeros_like(factor)
    for i, j in upper(nb):
        @pl.when((gy == j) & (gz == i))
        def _():
            factor[...] = r[i * B:(i + 1) * B, j * B:(j + 1) * B].T * scale
    for cp in cps:
        cp.wait()


def per_device(sizes, field, start_basis):
    n_gx, n_gy, n_gz = sizes
    planes, rows, species, width = field.shape
    n, rank = start_basis.shape
    quarter = species // n_gy
    chunks = planes * quarter
    nb = n // B
    total = len(above(nb)) * B
    columns = planes * n_gx * species * width * n_gz
    n_g = total // 4 // n_gx
    others = 2 * n_gx - 1
    n_sems = 1 + others + (n_gy - 1) + 1 + others + (n_gy - 1) + 2 * (2 * others + 1)
    rows_d = B // (4 * n_gx)
    packed, diagonal, reg = pl.pallas_call(
        functools.partial(gram_kernel, sizes),
        out_shape=(
            jax.ShapeDtypeStruct((total, B), F32),
            jax.ShapeDtypeStruct((n_gy, 4 * n_gx, rows_d, B), F32),
            jax.ShapeDtypeStruct((chunks, n, width), F32),
        ),
        in_specs=[HBM],
        out_specs=(VMEM, VMEM, VMEM),
        scratch_shapes=[
            pltpu.VMEM((total, B), F32),
            pltpu.VMEM((n, n), F32),
            pltpu.VMEM((total // 2, B), F32),
            pltpu.VMEM((2 * n_gx - 1, n_g, B), F32),
            pltpu.VMEM((n_gy - 1, n_g, B), F32),
            pltpu.VMEM((planes * species, rows, width), F32),
            pltpu.VMEM((B, B), F32),
            pltpu.VMEM((4 * n_gx, rows_d, B), F32),
            pltpu.VMEM((2 * n_gx, rows_d, B), F32),
            pltpu.VMEM((others, rows_d, B), F32),
            pltpu.SemaphoreType.DMA((2, n_sems)),
            pltpu.SemaphoreType.DMA((chunks, n_gy - 1)),
            pltpu.SemaphoreType.DMA((chunks, n_gy - 1)),
            pltpu.SemaphoreType.DMA((chunks,)),
            pltpu.SemaphoreType.DMA((planes * species,)),
        ],
        compiler_params=pltpu.CompilerParams(
            collective_id=0, has_side_effects=True, vmem_limit_bytes=32 << 20
        ),
        name="gram",
    )(field)
    basis_t, started = pl.pallas_call(
        basis_kernel,
        out_shape=(
            jax.ShapeDtypeStruct((rank, n), F32),
            jax.ShapeDtypeStruct((n, n), F32),
        ),
        in_specs=[VMEM, VMEM, VMEM],
        out_specs=(VMEM, VMEM),
        scratch_shapes=[
            pltpu.VMEM((n, n), F32),
            pltpu.VMEM((B, 2 * B), F32),
            pltpu.VMEM((B, 2 * B), F32),
        ],
        compiler_params=pltpu.CompilerParams(vmem_limit_bytes=32 << 20),
        name="solve",
    )(packed, diagonal, start_basis)
    core, factor = pl.pallas_call(
        functools.partial(core_kernel, n_gy, columns),
        out_shape=(
            jax.ShapeDtypeStruct((planes, species, rank // n_gy, width), F32),
            jax.ShapeDtypeStruct((n // n_gy, n // n_gz), F32),
        ),
        in_specs=[VMEM, VMEM, VMEM],
        out_specs=(VMEM, VMEM),
        scratch_shapes=[
            pltpu.VMEM((n, n), F32),
            pltpu.VMEM((B, 2 * B), F32),
            pltpu.VMEM((n_gy, planes, quarter, rank // n_gy, width), F32),
            pltpu.SemaphoreType.DMA((planes, n_gy - 1)),
            pltpu.SemaphoreType.DMA((planes, n_gy - 1)),
            pltpu.SemaphoreType.DMA((planes,)),
        ],
        compiler_params=pltpu.CompilerParams(
            collective_id=1, has_side_effects=True, vmem_limit_bytes=32 << 20
        ),
        name="core",
    )(basis_t, reg, started)
    return factor, jnp.transpose(core, (0, 2, 1, 3))


def solution(mesh):
    sizes = tuple(mesh.shape[a] for a in ("gx", "gy", "gz"))
    return jax.shard_map(
        functools.partial(per_device, sizes),
        mesh=mesh,
        in_specs=(P("gx", "gy", None, "gz"), P()),
        out_specs=(P("gy", "gz"), P("gx", "gy", None, "gz")),
        check_vma=False,
    )
```
